32 devices in a mesh: row: 8 (over y, x, core), col: 4 (over z).
Axes of the slice: x: 2, y: 2, z: 4, core: 2. Of those that a mesh axis runs over, the one named last changes fastest.
Arguments:
- solution: float32 [64, 32768], P(None, ('row', 'col')), may hold values from -6 to 6
- residual: float32 [64, 65536], P(None, ('row', 'col')), may hold values from -6 to 6
- direction: float32 [64, 32768], P(None, ('row', 'col')), may hold values from -6 to 6
- jacobian_tiles: bfloat16 [512, 20, 128, 128], P('row', 'col'), may hold values from -0.125 to 0.125
- tile_blocks: int32 [512, 20], P('row', 'col'), may hold values from 0 to 63, as said below
- tile_counts: int32 [512, 4], P('row', 'col'), may hold values from 1 to 5, as said below
Outputs:
- solution_next: float32 [64, 32768], P(None, ('row', 'col'))
- residual_next: float32 [64, 65536], P(None, ('row', 'col'))
- direction_next: float32 [64, 32768], P(None, ('row', 'col'))
The draws below stay inside these ranges and needn't reach their ends.
Inputs may be any that keep to these rules, and one draw needn't show every extreme that they name: `tile_blocks`: within each sensor and parameter group the 5 entries are different. Only the first tile_counts[i, c] slots of sensor i in group c hold a tile; some sensor fills all 5 slots of every group.
All inputs are finite; a program needn't handle non-finite values.
Results may differ from the reference program's by a relative error of at most 0.023.
Values may be sent and summed in bfloat16 or wider, within the bound.
No kernel may reach another device: no remote copies, remote signals or barrier semaphores. Data moves between devices by JAX's collectives and lax.ppermute only.
A program may use at most 128 MiB of HBM per device.

```python
import jax
import jax.numpy as jnp
from jax import lax

TB = 128
NRHS = 64
CB_DEV = 64
SLOT = 5
ITERS = 2
RB_DEV = 64
NRB = 512
NROWS = 65536
NPB = 256
NPAR = 32768
SHARD_BLOCKS = 8
N_ROW = 8
N_COL = 4


def draw_tile_blocks(key, part):
    groups = NPB // CB_DEV
    base = jax.random.fold_in(key, 3)
    subkeys = jax.random.split(base, NRB * groups)

    def choose_blocks(subkey):
        return jax.random.permutation(subkey, CB_DEV)[:SLOT]
    picks = jax.vmap(choose_blocks)(subkeys)
    return picks.reshape(NRB, groups * SLOT).astype(jnp.int32)


def draw_tile_counts(key, part):
    groups = NPB // CB_DEV
    base = jax.random.fold_in(key, 5)
    values = jax.random.randint(base, (NRB, groups), 1, SLOT + 1)
    chosen = jax.random.randint(jax.random.fold_in(base, 11), (), 0, NRB)
    marker = (jnp.arange(NRB) == chosen)[:, None]
    return jnp.where(marker, SLOT, values).astype(jnp.int32)


def levels(key, dims, shards, smallest, largest):
    def one(dim, shards_of):
        draws = jax.random.uniform(jax.random.fold_in(jax.random.fold_in(key, 6), dim), (shards_of,), jnp.float32, smallest / len(shards), largest / len(shards))
        return jnp.repeat(jnp.exp(draws), dims[dim] // shards_of).reshape((-1,) + (1,) * (len(dims) - dim - 1))

    loudness = one(*shards[0])
    for cut in shards[1:]:
        loudness = loudness * one(*cut)
    return loudness


def normal_values(rng, extent, width, limit, cuts=(), kind=jnp.bfloat16):
    level = levels(rng, extent, cuts, -0.22, 0.18) if cuts else 1.0
    array = jax.random.normal(rng, extent, jnp.float32) * width * level
    return jnp.minimum(jnp.maximum(array, -limit), limit).astype(kind)


def setup_inputs(seed: int = 0) -> dict:
    seeds = jax.random.split(jax.random.key(seed), 7)
    solution = normal_values(seeds[0], (NRHS, NPAR), 1.0, 6.0, ((1, 32),), jnp.float32)
    residual = normal_values(seeds[1], (NRHS, NROWS), 1.0, 6.0, ((1, 32),), jnp.float32)
    direction = normal_values(seeds[2], (NRHS, NPAR), 1.0, 6.0, ((1, 32),), jnp.float32)
    jacobian_tiles = normal_values(seeds[3], (NRB, N_COL * SLOT, TB, TB), (TB * SLOT * N_COL) ** -0.5, 0.125, ((0, 8), (1, 4)))
    tile_blocks = draw_tile_blocks(jax.random.fold_in(seeds[6], 71), 0)
    tile_counts = draw_tile_counts(jax.random.fold_in(seeds[6], 71), 0)
    return {"solution": solution, "residual": residual, "direction": direction, "jacobian_tiles": jacobian_tiles, "tile_blocks": tile_blocks, "tile_counts": tile_counts}


def times_highest(left, right):
    return jnp.dot(left, right, precision=lax.Precision.HIGHEST)

def gram_matrix(values):
    return jnp.dot(values, values.T, precision=lax.Precision.HIGHEST)

def solve_spd(matrix, right):
    factor_low = jnp.linalg.cholesky(matrix)
    middle = lax.linalg.triangular_solve(factor_low, right, left_side=True, lower=True)
    return lax.linalg.triangular_solve(factor_low, middle, left_side=True, lower=True, transpose_a=True)

def block_index(tile_blocks):
    groups = NPB // CB_DEV
    slots = jnp.arange(groups * SLOT, dtype=jnp.int32)
    group_of = (slots // SLOT)[None, :]
    owner = tile_blocks // SHARD_BLOCKS
    within = tile_blocks % SHARD_BLOCKS
    return ((owner * groups + group_of) * SHARD_BLOCKS + within).astype(jnp.int32)

def live_mask(tile_counts):
    slots = jnp.arange(NPB // CB_DEV * SLOT, dtype=jnp.int32)
    limits = jnp.repeat(tile_counts, SLOT, axis=1)
    return (slots[None, :] % SLOT < limits).astype(jnp.float32)

def forward(jacobian_tiles, blocks, live_slot, direction_half):
    groups = NPB // CB_DEV
    table_view = direction_half.reshape(NRHS, NPB, TB)
    tile_sets = jacobian_tiles.reshape(N_ROW, RB_DEV, groups * SLOT, TB, TB)
    block_sets = blocks.reshape(N_ROW, RB_DEV, groups * SLOT)
    live_sets = live_slot.reshape(N_ROW, RB_DEV, groups * SLOT)

    def one_range(pieces):
        tile_blk, index_blk, live_blk = pieces
        picked = jnp.take(table_view, index_blk, axis=1).astype(jnp.float32) * live_blk[None, :, :, None]
        product = jnp.einsum('rjab,nrjb->nrja', tile_blk.astype(jnp.float32), picked)
        product = product.reshape(NRHS, RB_DEV, groups, SLOT, TB).sum(axis=3)
        rounded = product.astype(jnp.bfloat16).astype(jnp.float32)
        return rounded.sum(axis=2).reshape(NRHS, RB_DEV * TB)
    ranges = lax.map(one_range, (tile_sets, block_sets, live_sets))
    return ranges.transpose(1, 0, 2).reshape(NRHS, NROWS)

def backward(jacobian_tiles, blocks, live_slot, rows_half):
    groups = NPB // CB_DEV
    row_sets = rows_half.reshape(NRHS, N_ROW, RB_DEV, TB).transpose(1, 0, 2, 3)
    tile_sets = jacobian_tiles.reshape(N_ROW, RB_DEV, groups * SLOT, TB, TB)
    block_sets = blocks.reshape(N_ROW, RB_DEV, groups * SLOT)
    live_sets = live_slot.reshape(N_ROW, RB_DEV, groups * SLOT)

    def one_range(running, pieces):
        tile_blk, index_blk, live_blk, row_blk = pieces
        contrib = jnp.einsum('rjab,nra->rjnb', tile_blk.astype(jnp.float32), row_blk.astype(jnp.float32))
        contrib = contrib * live_blk[:, :, None, None]
        added = jax.ops.segment_sum(contrib.reshape(-1, NRHS, TB), index_blk.reshape(-1), num_segments=NPB)
        return (running + added, None)
    start = jnp.zeros((NPB, NRHS, TB), jnp.float32)
    running, _ = lax.scan(one_range, start, (tile_sets, block_sets, live_sets, row_sets))
    return running.transpose(1, 0, 2).reshape(NRHS, NPAR)

def reference(solution, residual, direction, jacobian_tiles, tile_blocks, tile_counts):
    blocks = block_index(tile_blocks)
    live_slot = live_mask(tile_counts)
    gradient = backward(jacobian_tiles, blocks, live_slot, residual.astype(jnp.bfloat16))
    gamma_now = gram_matrix(gradient)
    for iteration in range(ITERS):
        image = forward(jacobian_tiles, blocks, live_slot, direction.astype(jnp.bfloat16))
        curvature = gram_matrix(image)
        step_alpha = solve_spd(curvature, gamma_now)
        solution = solution + times_highest(step_alpha.T, direction)
        residual = residual - times_highest(step_alpha.T, image)
        gradient = backward(jacobian_tiles, blocks, live_slot, residual.astype(jnp.bfloat16))
        gamma_next = gram_matrix(gradient)
        step_beta = solve_spd(gamma_now, gamma_next)
        direction = gradient + times_highest(step_beta.T, direction)
        gamma_now = gamma_next
    return (solution, residual, direction)
```

```python
import functools

import jax
import jax.numpy as jnp
from jax import lax
from jax.experimental import pallas as pl
from jax.experimental.pallas import tpu as pltpu
from jax.sharding import PartitionSpec as P

CHUNK = 8


def times_highest(left, right):
    return jnp.dot(left, right, precision=lax.Precision.HIGHEST)


def gram_matrix(values):
    return lax.dot_general(
        values,
        values,
        (((1,), (1,)), ((), ())),
        precision=lax.Precision.HIGHEST,
        preferred_element_type=jnp.float32,
    )


def gram_half(values):
    return lax.dot_general(
        values, values, (((1,), (1,)), ((), ())), preferred_element_type=jnp.float32
    )


def solve_kernel(matrix_ref, right_ref, out_ref):
    size = matrix_ref.shape[0]
    work = jnp.concatenate([matrix_ref[...], right_ref[...]], axis=1)
    rows = lax.broadcasted_iota(jnp.int32, (size, 1), 0)
    for k in range(size):
        pivot_row = work[k : k + 1, :]
        column = work[:, k : k + 1]
        pivot = work[k : k + 1, k : k + 1]
        scaled = pivot_row / pivot
        work = jnp.where(rows == k, scaled, work - column * scaled)
    out_ref[...] = work[:, size:]


def solve_spd(matrix, right):
    return pl.pallas_call(
        solve_kernel,
        out_shape=jax.ShapeDtypeStruct(right.shape, jnp.float32),
        name="spd_solve",
    )(matrix, right)


def image_kernel(where_ref, *refs, shards, slots, blocks_per):
    table_refs = refs[:shards]
    tiles_ref, out_ref, table_ref = refs[shards:]
    step = pl.program_id(0)
    tile = tiles_ref.shape[-1]
    total = shards * blocks_per

    @pl.when(step == 0)
    def _():
        for shard in range(shards):
            table_ref[shard] = table_refs[shard][...]

    for local in range(CHUNK):
        pieces = []
        tiles = []
        for slot in range(slots):
            place = where_ref[(step * CHUNK + local) * slots + slot]
            live = place < total
            spot = jnp.where(live, place, 0)
            piece = table_ref[
                spot // blocks_per,
                :,
                pl.ds(pl.multiple_of((spot % blocks_per) * tile, tile), tile),
            ]
            pieces.append(jnp.where(live, piece, jnp.zeros_like(piece)))
            tiles.append(tiles_ref[local, slot])
        product = lax.dot_general(
            jnp.concatenate(pieces, axis=1),
            jnp.concatenate(tiles, axis=1),
            (((1,), (1,)), ((), ())),
            preferred_element_type=jnp.float32,
        )
        out_ref[:, local * tile : (local + 1) * tile] = product.astype(out_ref.dtype)


def images(where_to, table, tiles):
    sensors, slots, tile, _ = tiles.shape
    shards = len(table)
    rhs, width = table[0].shape
    grid_spec = pltpu.PrefetchScalarGridSpec(
        num_scalar_prefetch=1,
        grid=(sensors // CHUNK,),
        in_specs=[pl.BlockSpec((rhs, width), lambda i, w: (0, 0)) for _ in table]
        + [pl.BlockSpec((CHUNK, slots, tile, tile), lambda i, w: (i, 0, 0, 0))],
        out_specs=pl.BlockSpec((rhs, CHUNK * tile), lambda i, w: (0, i)),
        scratch_shapes=[pltpu.VMEM((shards, rhs, width), jnp.bfloat16)],
    )
    return pl.pallas_call(
        functools.partial(
            image_kernel, shards=shards, slots=slots, blocks_per=width // tile
        ),
        grid_spec=grid_spec,
        out_shape=jax.ShapeDtypeStruct((rhs, sensors * tile), jnp.bfloat16),
        name="images",
    )(where_to, *table, tiles)


def gradient_kernel(
    where_ref, rows_ref, tiles_ref, keep_ref, send_ref, sums_ref, *, slots, blocks_per
):
    step = pl.program_id(0)
    tile = tiles_ref.shape[-1]

    @pl.when(step == 0)
    def _():
        sums_ref[...] = jnp.zeros_like(sums_ref)

    for local in range(CHUNK):
        rows = rows_ref[:, local * tile : (local + 1) * tile]
        tiles = jnp.concatenate([tiles_ref[local, slot] for slot in range(slots)], axis=1)
        product = jnp.dot(rows, tiles, preferred_element_type=jnp.float32)
        spots = [where_ref[(step * CHUNK + local) * slots + slot] for slot in range(slots)]
        olds = [sums_ref[spot] for spot in spots]
        for slot in range(slots):
            sums_ref[spots[slot]] = (
                olds[slot] + product[:, slot * tile : (slot + 1) * tile]
            )

    @pl.when(step == pl.num_programs(0) - 1)
    def _():
        for shard in range(keep_ref.shape[0]):
            for block in range(blocks_per):
                span = slice(block * tile, (block + 1) * tile)
                keep_ref[shard, :, span] = sums_ref[2 * shard * blocks_per + block]
                send_ref[shard, :, span] = sums_ref[
                    (2 * shard + 1) * blocks_per + block
                ].astype(send_ref.dtype)


def gradients(where_to, rows, tiles, shards, width):
    sensors, slots, tile, _ = tiles.shape
    rhs = rows.shape[0]
    half = shards // 2
    grid_spec = pltpu.PrefetchScalarGridSpec(
        num_scalar_prefetch=1,
        grid=(sensors // CHUNK,),
        in_specs=[
            pl.BlockSpec((rhs, CHUNK * tile), lambda i, w: (0, i)),
            pl.BlockSpec((CHUNK, slots, tile, tile), lambda i, w: (i, 0, 0, 0)),
        ],
        out_specs=[
            pl.BlockSpec((half, rhs, width), lambda i, w: (0, 0, 0)),
            pl.BlockSpec((half, rhs, width), lambda i, w: (0, 0, 0)),
        ],
        scratch_shapes=[
            pltpu.VMEM((shards * width // tile + 1, rhs, tile), jnp.float32)
        ],
    )
    return pl.pallas_call(
        functools.partial(gradient_kernel, slots=slots, blocks_per=width // tile),
        grid_spec=grid_spec,
        out_shape=[
            jax.ShapeDtypeStruct((half, rhs, width), jnp.float32),
            jax.ShapeDtypeStruct((half, rhs, width), jnp.bfloat16),
        ],
        name="gradients",
    )(where_to, rows, tiles)


def per_device(
    solution, residual, direction, jacobian_tiles, tile_blocks, tile_counts, *, n_row, n_col
):
    rhs, width = direction.shape
    tile = jacobian_tiles.shape[2]
    slots = jacobian_tiles.shape[1]
    blocks_per = width // tile
    me = lax.axis_index("row")
    odd = (me & 1) == 1
    low, high = n_row // 4, n_row // 2

    def swap(value, mask, axis="row"):
        size = n_row if axis == "row" else n_col
        return lax.ppermute(value, axis, [(i, i ^ mask) for i in range(size)])

    def swap_mixed(value):
        return lax.ppermute(
            value, "row", [(i, i ^ (high if i & 1 else low)) for i in range(n_row)]
        )

    def sum_row(value):
        mask = 1
        while mask < n_row:
            value = value + swap(value, mask)
            mask *= 2
        return value

    def sum_all(value):
        value = sum_row(value)
        mask = 1
        while mask < n_col:
            value = value + swap(value, mask, "col")
            mask *= 2
        return value

    def gather_row(value):
        held = {0: value, low: swap(value, low), high: swap(value, high)}
        held[low | high] = swap_mixed(jnp.where(odd, held[low], held[high]))
        mask = low // 2
        while mask:
            for j in list(held):
                held[j ^ mask] = swap(held[j], mask)
            mask //= 2
        return [held[j] for j in range(n_row)]

    def scatter_row(parts):
        keep, send = parts
        got = swap(send, 1)
        held = {2 * j: keep[j] + got[j].astype(jnp.float32) for j in range(n_row // 2)}
        mask = 2
        while mask < low:
            for j in [j for j in held if j & mask]:
                moved = swap(held.pop(j).astype(jnp.bfloat16), mask)
                held[j ^ mask] = held[j ^ mask] + moved.astype(jnp.float32)
            mask *= 2
        cross = swap_mixed(held[low | high].astype(jnp.bfloat16)).astype(jnp.float32)
        to_low = (held[low] + jnp.where(odd, cross, 0.0)).astype(jnp.bfloat16)
        to_high = (held[high] + jnp.where(odd, 0.0, cross)).astype(jnp.bfloat16)
        return (
            held[0]
            + swap(to_low, low).astype(jnp.float32)
            + swap(to_high, high).astype(jnp.float32)
        )

    owner = (tile_blocks // blocks_per) ^ me
    live = jnp.arange(slots, dtype=jnp.int32)[None, :] < tile_counts
    where_to = jnp.where(
        live, owner * blocks_per + tile_blocks % blocks_per, n_row * blocks_per
    ).reshape(-1)

    def image_of(value):
        table = gather_row(value.astype(jnp.bfloat16))
        return lax.psum(images(where_to, table, jacobian_tiles), "col")

    def gradient_of(rows):
        return scatter_row(gradients(where_to, rows, jacobian_tiles, n_row, width))

    rows_half = lax.all_gather(residual.astype(jnp.bfloat16), "col", axis=1, tiled=True)
    image_first = image_of(direction)
    gradient = gradient_of(rows_half)
    gamma = sum_all(gram_matrix(gradient))

    curvature = sum_row(gram_half(image_first))
    change = gradient_of(image_first)
    alpha = solve_spd(curvature, gamma)
    gradient = gradient - times_highest(alpha.T, change)

    image_part = image_of(gradient)
    gamma_next = sum_all(gram_matrix(gradient))
    beta = solve_spd(gamma, gamma_next)
    image = image_part.astype(jnp.float32) + times_highest(
        beta.T, image_first.astype(jnp.float32)
    )
    iterate = solution + times_highest(alpha.T, direction)
    direction = gradient + times_highest(beta.T, direction)
    share_rows = residual.shape[1]
    start = lax.axis_index("col") * share_rows

    def share(value):
        return lax.dynamic_slice_in_dim(value, start, share_rows, 1).astype(jnp.float32)

    remaining = residual - times_highest(alpha.T, share(image_first))
    gamma = gamma_next

    image_half = image.astype(jnp.bfloat16)
    curvature = sum_row(gram_half(image_half))
    change = gradient_of(image_half)
    alpha = solve_spd(curvature, gamma)
    inverse = solve_spd(gamma, jnp.eye(rhs, dtype=jnp.float32))
    weighted = times_highest(inverse, direction)
    gradient = gradient - times_highest(alpha.T, change)
    gamma_next = sum_all(gram_matrix(gradient))
    iterate = iterate + times_highest(alpha.T, direction)
    remaining = remaining - times_highest(alpha.T, share(image))
    direction = gradient + times_highest(gamma_next, weighted)
    return (iterate, remaining, direction)


def solution(mesh):
    vector = P(None, ("row", "col"))
    placed = (
        vector,
        vector,
        vector,
        P("row", "col", None, None),
        P("row", "col"),
        P("row", "col"),
    )
    return jax.shard_map(
        functools.partial(per_device, n_row=mesh.shape["row"], n_col=mesh.shape["col"]),
        mesh=mesh,
        in_specs=placed,
        out_specs=(vector, vector, vector),
        check_vma=False,
    )
```

```python
import functools

import jax
import jax.numpy as jnp
from jax import lax
from jax.experimental import pallas as pl
from jax.experimental.pallas import tpu as pltpu
from jax.sharding import PartitionSpec as P

UNROLL = 8
IN_VMEM = pl.BlockSpec(memory_space=pltpu.VMEM)
IN_SMEM = pl.BlockSpec(memory_space=pltpu.SMEM)
PARAMS = pltpu.CompilerParams(vmem_limit_bytes=24 * 2**20)


def times_highest(left, right):
    return jnp.dot(left, right, precision=lax.Precision.HIGHEST)


def gram_matrix(values):
    return lax.dot_general(
        values,
        values,
        (((1,), (1,)), ((), ())),
        precision=lax.Precision.HIGHEST,
        preferred_element_type=jnp.float32,
    )


def solve_kernel(matrix_ref, right_ref, out_ref):
    size = matrix_ref.shape[0]
    work = jnp.concatenate([matrix_ref[...], right_ref[...]], axis=1)
    rows = lax.broadcasted_iota(jnp.int32, (size, 1), 0)
    for k in range(size):
        scaled = work[k : k + 1, :] / work[k : k + 1, k : k + 1]
        work = jnp.where(rows == k, scaled, work - work[:, k : k + 1] * scaled)
    out_ref[...] = work[:, size:]


def solve_spd(matrix, right):
    return pl.pallas_call(
        solve_kernel,
        out_shape=jax.ShapeDtypeStruct(right.shape, jnp.float32),
        name="spd_solve",
    )(matrix, right)


def tile_span(index, tile):
    return pl.ds(pl.multiple_of(index * tile, tile), tile)


def image_kernel(place_ref, start_ref, *refs, parts, first):
    table_refs = refs[: len(refs) - parts - 1 - first]
    tiles_ref = refs[len(table_refs)]
    out_refs = refs[len(table_refs) + 1 + first :]
    if first:
        table_ref = refs[len(table_refs) + 1]
        for shard, shard_ref in enumerate(table_refs):
            table_ref[shard] = shard_ref[...]
    else:
        table_ref = table_refs[0]
    slots, tile = tiles_ref.shape[1], tiles_ref.shape[2]
    blocks_per = table_ref.shape[2] // tile
    total = table_ref.shape[0] * blocks_per

    for part, out_ref in enumerate(out_refs):
        sensors = out_ref.shape[1] // tile
        unroll = min(UNROLL, sensors)

        def some(step, carry, part=part, out_ref=out_ref, unroll=unroll):
            for local in range(unroll):
                near = step * unroll + local
                sensor = start_ref[part] + near
                pieces, tiles = [], []
                for slot in range(slots):
                    place = place_ref[sensor * slots + slot]
                    live = place < total
                    spot = jnp.where(live, place, 0)
                    piece = table_ref[
                        spot // blocks_per, :, tile_span(spot % blocks_per, tile)
                    ]
                    pieces.append(jnp.where(live, piece, jnp.zeros_like(piece)))
                    tiles.append(tiles_ref[sensor, slot])
                product = lax.dot_general(
                    jnp.concatenate(tiles, axis=1),
                    jnp.concatenate(pieces, axis=1),
                    (((1,), (1,)), ((), ())),
                    preferred_element_type=jnp.float32,
                )
                out_ref[:, tile_span(near, tile)] = product.T.astype(out_ref.dtype)
            return carry

        lax.fori_loop(0, sensors // unroll, some, 0)


def images(place, starts, table, tiles, dtypes, count):
    parts = starts.shape[0]
    first = isinstance(table, list)
    shards = table if first else [table]
    rhs, width = shards[0].shape[-2:]
    sensors, slots, tile, _ = tiles.shape
    columns = sensors // count * tile
    out = [jax.ShapeDtypeStruct((rhs, columns), dtype) for dtype in dtypes]
    if first:
        out = [jax.ShapeDtypeStruct((len(shards), rhs, width), jnp.bfloat16)] + out
    return pl.pallas_call(
        functools.partial(image_kernel, parts=parts, first=first),
        in_specs=[IN_SMEM, IN_SMEM] + [IN_VMEM] * (len(shards) + 1),
        out_specs=[IN_VMEM] * len(out),
        out_shape=out,
        compiler_params=PARAMS,
        name="images",
    )(place, starts, *shards, tiles)


def gradient_kernel(place_ref, start_ref, *refs, parts, first):
    row_refs = refs[:parts]
    tiles_ref = refs[parts]
    if first:
        sums_ref = refs[parts + 1]
        sums_ref[...] = jnp.zeros_like(sums_ref)
    else:
        sums_ref, keep_ref, send_ref = refs[parts + 2 :]
    slots, tile = tiles_ref.shape[1], tiles_ref.shape[2]

    for part, row_ref in enumerate(row_refs):
        sensors = row_ref.shape[1] // tile
        unroll = min(UNROLL, sensors)

        def some(step, carry, part=part, row_ref=row_ref, unroll=unroll):
            for local in range(unroll):
                near = step * unroll + local
                sensor = start_ref[part] + near
                tiles = [tiles_ref[sensor, slot] for slot in range(slots)]
                product = jnp.dot(
                    row_ref[:, tile_span(near, tile)],
                    jnp.concatenate(tiles, axis=1),
                    preferred_element_type=jnp.float32,
                )
                spots = [place_ref[sensor * slots + slot] for slot in range(slots)]
                olds = [sums_ref[spot] for spot in spots]
                for slot in range(slots):
                    sums_ref[spots[slot]] = (
                        olds[slot] + product[:, slot * tile : (slot + 1) * tile]
                    )
            return carry

        lax.fori_loop(0, sensors // unroll, some, 0)

    if not first:
        blocks_per = keep_ref.shape[2] // tile
        for shard in range(keep_ref.shape[0]):
            for block in range(blocks_per):
                span = slice(block * tile, (block + 1) * tile)
                keep_ref[shard, :, span] = sums_ref[2 * shard * blocks_per + block]
                send_ref[shard, :, span] = sums_ref[
                    (2 * shard + 1) * blocks_per + block
                ].astype(send_ref.dtype)


def gradients_first(place, starts, rows, tiles, blocks):
    rhs, tile = rows[0].shape[0], tiles.shape[2]
    return pl.pallas_call(
        functools.partial(gradient_kernel, parts=len(rows), first=True),
        in_specs=[IN_SMEM, IN_SMEM] + [IN_VMEM] * (len(rows) + 1),
        out_specs=IN_VMEM,
        out_shape=jax.ShapeDtypeStruct((blocks + 1, rhs, tile), jnp.float32),
        compiler_params=PARAMS,
        name="gradients_first",
    )(place, starts, *rows, tiles)


def gradients_last(place, starts, rows, tiles, sums, shards, width):
    rhs = rows[0].shape[0]
    half = (shards // 2, rhs, width)
    _, keep, send = pl.pallas_call(
        functools.partial(gradient_kernel, parts=len(rows), first=False),
        in_specs=[IN_SMEM, IN_SMEM] + [IN_VMEM] * (len(rows) + 2),
        out_specs=[IN_VMEM] * 3,
        out_shape=[
            jax.ShapeDtypeStruct(sums.shape, jnp.float32),
            jax.ShapeDtypeStruct(half, jnp.float32),
            jax.ShapeDtypeStruct(half, jnp.bfloat16),
        ],
        input_output_aliases={len(rows) + 3: 0},
        compiler_params=PARAMS,
        name="gradients_last",
    )(place, starts, *rows, tiles, sums)
    return keep, send


def per_device(
    solution, residual, direction, jacobian_tiles, tile_blocks, tile_counts, *, n_row, n_col
):
    rhs, width = direction.shape
    sensors, slots, tile, _ = jacobian_tiles.shape
    blocks_per = width // tile
    my_row = lax.axis_index("row")
    my_col = lax.axis_index("col")
    chips = range(2, n_row, 2)
    far = range(n_col - 1, 1, -1)

    def swap_row(value, mask):
        return lax.ppermute(value, "row", [(i, i ^ mask) for i in range(n_row)])

    def swap_col(value, mask):
        return lax.ppermute(value, "col", [(i, i ^ mask) for i in range(n_col)])

    def add_up(values):
        while len(values) > 1:
            values = [a + b for a, b in zip(values[::2], values[1::2])] + (
                values[-1:] if len(values) % 2 else []
            )
        return values[0]

    def sum_row(value):
        value = value + swap_row(value, 1)
        return add_up([value] + [swap_row(value, mask) for mask in chips])

    def sum_all(value):
        value = sum_row(value)
        return add_up([value] + [swap_col(value, mask) for mask in range(1, n_col)])

    def gather_row(value):
        held = {0: value}
        for mask in chips:
            held[mask] = swap_row(value, mask)
        for mask in list(held):
            held[mask ^ 1] = swap_row(held[mask], 1)
        return [held[j] for j in range(n_row)]

    def scatter_row(parts):
        keep, send = parts
        got = swap_row(send, 1)
        held = [keep[j] + got[j].astype(jnp.float32) for j in range(n_row // 2)]
        moved = [swap_row(held[m // 2].astype(jnp.bfloat16), m) for m in chips]
        return add_up([held[0]] + [value.astype(jnp.float32) for value in moved])

    owner = (tile_blocks // blocks_per) ^ my_row
    live = jnp.arange(slots, dtype=jnp.int32)[None, :] < tile_counts
    place = jnp.where(
        live, owner * blocks_per + tile_blocks % blocks_per, n_row * blocks_per
    ).reshape(-1)
    starts = (my_col ^ jnp.arange(n_col, dtype=jnp.int32)) * (sensors // n_col)
    far_starts = starts[:1:-1]
    near_starts = starts[1::-1]

    def image_share(value):
        shards = gather_row(value.astype(jnp.bfloat16))
        table, *parts = images(
            place, far_starts, shards, jacobian_tiles, [jnp.bfloat16] * len(far), n_col
        )
        parts = [swap_col(part, mask) for part, mask in zip(parts, far)]
        next_part, own = images(
            place, near_starts, table, jacobian_tiles, [jnp.bfloat16, jnp.float32], n_col
        )
        parts = [own, swap_col(next_part, 1)] + parts
        return add_up([part.astype(jnp.float32) for part in parts])

    def gradient_of(share):
        half = share.astype(jnp.bfloat16)
        away = [swap_col(half, mask) for mask in far]
        sums = gradients_first(
            place, near_starts, [swap_col(half, 1), half], jacobian_tiles, n_row * blocks_per
        )
        return scatter_row(
            gradients_last(place, far_starts, away, jacobian_tiles, sums, n_row, width)
        )

    image_first = image_share(direction)
    gradient = gradient_of(residual)
    gamma = sum_all(gram_matrix(gradient))

    curvature = sum_all(gram_matrix(image_first))
    change = gradient_of(image_first)
    alpha = solve_spd(curvature, gamma)
    gradient = gradient - times_highest(alpha.T, change)

    image_part = image_share(gradient)
    gamma_next = sum_all(gram_matrix(gradient))
    beta = solve_spd(gamma, gamma_next)
    image = image_part + times_highest(beta.T, image_first)
    iterate = solution + times_highest(alpha.T, direction)
    direction = gradient + times_highest(beta.T, direction)
    remaining = residual - times_highest(alpha.T, image_first)
    gamma = gamma_next

    curvature = sum_all(gram_matrix(image))
    change = gradient_of(image)
    alpha = solve_spd(curvature, gamma)
    inverse = solve_spd(gamma, jnp.eye(rhs, dtype=jnp.float32))
    weighted = times_highest(inverse, direction)
    gradient = gradient - times_highest(alpha.T, change)
    gamma_next = sum_all(gram_matrix(gradient))
    iterate = iterate + times_highest(alpha.T, direction)
    remaining = remaining - times_highest(alpha.T, image)
    direction = gradient + times_highest(gamma_next, weighted)
    return (iterate, remaining, direction)


def solution(mesh):
    vector = P(None, ("row", "col"))
    placed = (
        vector,
        vector,
        vector,
        P("row", "col", None, None),
        P("row", "col"),
        P("row", "col"),
    )
    return jax.shard_map(
        functools.partial(per_device, n_row=mesh.shape["row"], n_col=mesh.shape["col"]),
        mesh=mesh,
        in_specs=placed,
        out_specs=(vector, vector, vector),
        check_vma=False,
    )
```

```python
import functools

import jax
import jax.numpy as jnp
from jax import lax
from jax.experimental import pallas as pl
from jax.experimental.pallas import tpu as pltpu
from jax.sharding import PartitionSpec as P


UNROLL = 8
IN_VMEM = pl.BlockSpec(memory_space=pltpu.VMEM)
IN_SMEM = pl.BlockSpec(memory_space=pltpu.SMEM)
PARAMS = pltpu.CompilerParams(vmem_limit_bytes=16 * 2**20)


def times_highest(left, right):
    return jnp.dot(left, right, precision=lax.Precision.HIGHEST)


def gram_matrix(values):
    return lax.dot_general(
        values,
        values,
        (((1,), (1,)), ((), ())),
        precision=lax.Precision.HIGHEST,
        preferred_element_type=jnp.float32,
    )


def solve_kernel(matrix_ref, gamma_ref, solved_ref, inverse_ref):
    size = matrix_ref.shape[0]
    gamma = gamma_ref[...]
    rows = lax.broadcasted_iota(jnp.int32, (size, 1), 0)
    unit = (rows == lax.broadcasted_iota(jnp.int32, (size, size), 1)).astype(jnp.float32)
    works = [
        jnp.concatenate([matrix_ref[...], gamma], axis=1),
        jnp.concatenate([gamma, unit], axis=1),
    ]
    for k in range(size):
        for n, work in enumerate(works):
            scaled = work[k : k + 1, :] / work[k : k + 1, k : k + 1]
            works[n] = jnp.where(rows == k, scaled, work - work[:, k : k + 1] * scaled)
    solved_ref[...] = works[0][:, size:]
    inverse_ref[...] = works[1][:, size:]


def solve_spd(matrix, gamma):
    return pl.pallas_call(
        solve_kernel,
        out_shape=[jax.ShapeDtypeStruct(gamma.shape, jnp.float32)] * 2,
        compiler_params=pltpu.CompilerParams(vmem_limit_bytes=2 * 2**20),
        name="spd_solve",
    )(matrix, gamma)


def tile_span(index, tile):
    return pl.ds(pl.multiple_of(index * tile, tile), tile)


def token_kernel(tiles_ref, out_ref):
    del tiles_ref
    out_ref[...] = jnp.zeros_like(out_ref)


def hold_tiles(tiles):
    return pl.pallas_call(
        token_kernel,
        in_specs=[IN_VMEM],
        out_specs=IN_VMEM,
        out_shape=jax.ShapeDtypeStruct((8, tiles.shape[-1]), jnp.float32),
        compiler_params=PARAMS,
        name="hold_tiles",
    )(tiles)


def image_kernel(place_ref, *refs, parts, share, first):
    table_refs = refs[: len(refs) - len(parts) - 2 - first]
    tiles_ref = refs[len(table_refs)]
    out_refs = refs[len(table_refs) + 2 + first :]
    slots, tile = tiles_ref.shape[1], tiles_ref.shape[2]
    if first:
        table_ref = refs[len(table_refs) + 2]
        blocks_per = table_refs[0].shape[1] // tile
        for shard, shard_ref in enumerate(table_refs):
            for block in range(blocks_per):
                table_ref[shard * blocks_per + block] = shard_ref[
                    :, block * tile : (block + 1) * tile
                ]
        table_ref[table_ref.shape[0] - 1] = jnp.zeros_like(table_ref[0])
    else:
        table_ref = table_refs[0]

    for (mask, offset), out_ref in zip(parts, out_refs):
        sensors = out_ref.shape[1] // tile
        unroll = min(UNROLL, sensors)
        start = (lax.axis_index("col") ^ mask) * share + offset

        def some(step, carry, start=start, out_ref=out_ref, unroll=unroll):
            for local in range(unroll):
                near = step * unroll + local
                sensor = start + near
                places = [place_ref[sensor * slots + slot] for slot in range(slots)]
                pieces = [table_ref[place] for place in places]
                tiles = [tiles_ref[sensor, slot] for slot in range(slots)]
                product = lax.dot_general(
                    jnp.concatenate(tiles, axis=1),
                    jnp.concatenate(pieces, axis=1),
                    (((1,), (1,)), ((), ())),
                    preferred_element_type=jnp.float32,
                )
                out_ref[:, tile_span(near, tile)] = product.T.astype(out_ref.dtype)
            return carry

        lax.fori_loop(0, sensors // unroll, some, 0)


def images(place, table, tiles, token, parts, share):
    first = isinstance(table, list)
    shards = table if first else [table]
    tile = tiles.shape[2]
    rhs = shards[0].shape[-2]
    out = [jax.ShapeDtypeStruct((rhs, part[2] * tile), part[3]) for part in parts]
    if first:
        blocks = len(shards) * shards[0].shape[1] // tile
        out = [jax.ShapeDtypeStruct((blocks + 1, rhs, tile), jnp.bfloat16)] + out
    return pl.pallas_call(
        functools.partial(
            image_kernel, parts=[part[:2] for part in parts], share=share, first=first
        ),
        in_specs=[IN_SMEM] + [IN_VMEM] * (len(shards) + 2),
        out_specs=[IN_VMEM] * len(out),
        out_shape=out,
        compiler_params=PARAMS,
        name="images",
    )(place, *shards, tiles, token)


def gradient_kernel(place_ref, *refs, places, share, first):
    parts = len(places)
    row_refs = refs[:parts]
    tiles_ref = refs[parts]
    if first:
        sums_ref = refs[parts + 1]
        sums_ref[...] = jnp.zeros_like(sums_ref)
    else:
        sums_ref, keep_ref, send_ref = refs[parts + 2 :]
    slots, tile = tiles_ref.shape[1], tiles_ref.shape[2]

    for (mask, offset), row_ref in zip(places, row_refs):
        sensors = row_ref.shape[1] // tile
        unroll = min(UNROLL, sensors)
        start = (lax.axis_index("col") ^ mask) * share + offset

        def some(step, carry, start=start, row_ref=row_ref, unroll=unroll):
            for local in range(unroll):
                near = step * unroll + local
                sensor = start + near
                tiles = [tiles_ref[sensor, slot] for slot in range(slots)]
                product = jnp.dot(
                    row_ref[:, tile_span(near, tile)],
                    jnp.concatenate(tiles, axis=1),
                    preferred_element_type=jnp.float32,
                )
                spots = [place_ref[sensor * slots + slot] for slot in range(slots)]
                olds = [sums_ref[spot] for spot in spots]
                for slot in range(slots):
                    sums_ref[spots[slot]] = (
                        olds[slot] + product[:, slot * tile : (slot + 1) * tile]
                    )
            return carry

        lax.fori_loop(0, sensors // unroll, some, 0)

    if not first:
        blocks_per = keep_ref.shape[2] // tile
        for shard in range(keep_ref.shape[0]):
            for block in range(blocks_per):
                span = slice(block * tile, (block + 1) * tile)
                keep_ref[shard, :, span] = sums_ref[2 * shard * blocks_per + block]
                send_ref[shard, :, span] = sums_ref[
                    (2 * shard + 1) * blocks_per + block
                ].astype(send_ref.dtype)


def piece_places(held, masks, tile):
    places, pieces = [], []
    for mask in masks:
        offset = 0
        for piece in held[mask]:
            places.append((mask, offset))
            pieces.append(piece)
            offset += piece.shape[1] // tile
    return places, pieces


def gradients_first(place, held, masks, tiles, share, blocks):
    tile = tiles.shape[2]
    places, rows = piece_places(held, masks, tile)
    return pl.pallas_call(
        functools.partial(gradient_kernel, places=places, share=share, first=True),
        in_specs=[IN_SMEM] + [IN_VMEM] * (len(rows) + 1),
        out_specs=IN_VMEM,
        out_shape=jax.ShapeDtypeStruct((blocks + 1, rows[0].shape[0], tile), jnp.float32),
        compiler_params=PARAMS,
        name="gradients_first",
    )(place, *rows, tiles)


def gradients_last(place, held, masks, tiles, share, sums, shards, width):
    places, rows = piece_places(held, masks, tiles.shape[2])
    half = (shards // 2, rows[0].shape[0], width)
    _, keep, send = pl.pallas_call(
        functools.partial(gradient_kernel, places=places, share=share, first=False),
        in_specs=[IN_SMEM] + [IN_VMEM] * (len(rows) + 2),
        out_specs=[IN_VMEM] * 3,
        out_shape=[
            jax.ShapeDtypeStruct(sums.shape, jnp.float32),
            jax.ShapeDtypeStruct(half, jnp.float32),
            jax.ShapeDtypeStruct(half, jnp.bfloat16),
        ],
        input_output_aliases={len(rows) + 2: 0},
        compiler_params=PARAMS,
        name="gradients_last",
    )(place, *rows, tiles, sums)
    return keep, send


def per_device(
    solution, residual, direction, jacobian_tiles, tile_blocks, tile_counts, *, n_row, n_col
):
    rhs, width = direction.shape
    sensors, slots, tile, _ = jacobian_tiles.shape
    blocks_per = width // tile
    chips = range(2, n_row, 2)

    def swap_row(value, mask):
        return lax.ppermute(value, "row", [(i, i ^ mask) for i in range(n_row)])

    def swap_col(value, mask):
        return lax.ppermute(value, "col", [(i, i ^ mask) for i in range(n_col)])

    def add_up(values):
        while len(values) > 1:
            values = [a + b for a, b in zip(values[::2], values[1::2])] + (
                values[-1:] if len(values) % 2 else []
            )
        return values[0]

    def sum_all(value):
        value = value + swap_row(value, 1)
        values = [value]
        for mask in chips:
            values.append(swap_row(value, mask))
        value = add_up(values)
        values = [value]
        for mask in range(n_col - 1, 0, -1):
            values.append(swap_col(value, mask))
        return add_up(values)

    def gather_row(value):
        held = {0: value}
        for mask in chips:
            held[mask] = swap_row(value, mask)
        for mask in list(held):
            held[mask ^ 1] = swap_row(held[mask], 1)
        return [held[j] for j in range(n_row)]

    def scatter_row(parts):
        keep, send = parts
        got = swap_row(send, 1)
        held = [keep[j] + got[j].astype(jnp.float32) for j in range(n_row // 2)]
        moved = []
        for mask in chips:
            moved.append(swap_row(held[mask // 2].astype(jnp.bfloat16), mask))
        return add_up([held[0]] + [value.astype(jnp.float32) for value in moved])

    share = sensors // n_col
    far = tuple(range(n_col - 1, 1, -1))
    owner = (tile_blocks // blocks_per) ^ lax.axis_index("row")
    live = jnp.arange(slots, dtype=jnp.int32)[None, :] < tile_counts
    place = jnp.where(
        live, owner * blocks_per + tile_blocks % blocks_per, n_row * blocks_per
    ).reshape(-1)
    token = hold_tiles(jacobian_tiles)

    def halves(value):
        middle = value.shape[1] // 2
        return [value[:, :middle], value[:, middle:]]

    def image_share(value):
        shards = gather_row(value.astype(jnp.bfloat16))
        cuts = [(0, share // 2), (share // 2, share // 2)]
        odd = [(m, *cut, jnp.bfloat16) for m in far if m & 1 for cut in cuts]
        even = [(m, *cut, jnp.float32) for m in far if not m & 1 for cut in cuts]
        near = [(1, 0, share, jnp.bfloat16), (0, 0, share, jnp.float32)]
        table, *sent = images(place, shards, jacobian_tiles, token, odd, share)
        moved = {}
        for n, piece in enumerate(sent):
            moved[odd[n][:2]] = swap_col(piece, 1)
        *held, beside, own = images(
            place, table, jacobian_tiles, token, even + near, share
        )
        beside = swap_col(beside, 1)
        held = {
            part[:2]: piece + moved[part[0] ^ 1, part[1]].astype(jnp.float32)
            for part, piece in zip(even, held)
        }
        mask = 2
        ends = [None] * len(cuts)
        while mask < n_col:
            for m in [m for m in far if not m & 1 and m & mask and (m, 0) in held]:
                for n, cut in enumerate(cuts):
                    got = swap_col(held.pop((m, cut[0])).astype(jnp.bfloat16), mask)
                    got = got.astype(jnp.float32)
                    if m == mask:
                        ends[n] = got if ends[n] is None else ends[n] + got
                    else:
                        held[m ^ mask, cut[0]] = held[m ^ mask, cut[0]] + got
            mask *= 2
        return own + beside.astype(jnp.float32) + jnp.concatenate(ends, axis=1)

    def gather_col(value):
        half = value.astype(jnp.bfloat16)
        pieces = [piece.astype(jnp.bfloat16) for piece in halves(value)]
        held = {0: pieces}
        mask = n_col // 2
        while mask:
            for j in list(held):
                held[j ^ mask] = []
                for piece in [half] if mask == 1 and j == 0 else held[j]:
                    held[j ^ mask].append(swap_col(piece, mask))
            mask //= 2
        held[0] = [half]
        return held

    def gradient_of(value):
        held = gather_col(value)
        sums = gradients_first(
            place, held, (1, 0), jacobian_tiles, share, n_row * blocks_per
        )
        parts = gradients_last(
            place, held, far, jacobian_tiles, share, sums, n_row, width
        )
        return scatter_row(parts)

    gradient = gradient_of(residual)
    image_first = image_share(direction)
    curvature = gram_matrix(image_first)
    both = sum_all(jnp.concatenate([gram_matrix(gradient), curvature]))
    gamma, curvature = both[:rhs], both[rhs:]
    change = gradient_of(image_first)
    alpha, inverse = solve_spd(curvature, gamma)
    gradient = gradient - times_highest(alpha.T, change)

    image_part = image_share(gradient)
    gamma_next = sum_all(gram_matrix(gradient))
    beta = times_highest(inverse, gamma_next)
    image = image_part + times_highest(beta.T, image_first)
    iterate = solution + times_highest(alpha.T, direction)
    direction = gradient + times_highest(beta.T, direction)
    remaining = residual - times_highest(alpha.T, image_first)
    gamma = gamma_next

    curvature = gram_matrix(image)
    curvature = sum_all(curvature)
    change = gradient_of(image_part) + times_highest(
        beta.T, change
    )
    alpha, inverse = solve_spd(curvature, gamma)
    weighted = times_highest(inverse, direction)
    gradient = gradient - times_highest(alpha.T, change)
    gamma_next = sum_all(gram_matrix(gradient))
    iterate = iterate + times_highest(alpha.T, direction)
    remaining = remaining - times_highest(alpha.T, image)
    direction = gradient + times_highest(gamma_next, weighted)
    return (iterate, remaining, direction)


def solution(mesh):
    vector = P(None, ("row", "col"))
    placed = (
        vector,
        vector,
        vector,
        P("row", "col", None, None),
        P("row", "col"),
        P("row", "col"),
    )

    def body(*operands):
        return per_device(*operands, n_row=mesh.shape["row"], n_col=mesh.shape["col"])

    return jax.shard_map(
        body,
        mesh=mesh,
        in_specs=placed,
        out_specs=(vector, vector, vector),
        check_vma=False,
    )
```
